32 devices in a mesh: seq: 16 (over z, x, core), head: 2 (over y).
Axes of the slice: x: 2, y: 2, z: 4, core: 2. Of those that a mesh axis runs over, the one named last changes fastest.
Arguments:
- queries: bfloat16 [16384, 2048], P(('seq', 'head')), may hold values from -6 to 6
- key_rows: bfloat16 [16384, 2048], P(('seq', 'head')), may hold values from -6 to 6
- values: bfloat16 [16384, 4096], P(('seq', 'head')), may hold values from -140 to 140
- in_gate: bfloat16 [16384, 8], P(('seq', 'head')), may hold values from -6 to 226
- forget_gate: bfloat16 [16384, 8], P(('seq', 'head')), may hold values from -0.25 to 15
- out_gate: bfloat16 [16384, 4096], P(('seq', 'head')), may hold values from -6 to 6
- norm_gain: float32 [4096], P('head'), may hold values from 0.1 to 1.9
Outputs:
- layer_out: bfloat16 [16384, 4096], P(('seq', 'head'))
The draws below stay inside these ranges and needn't reach their ends.
All inputs are finite; a program needn't handle non-finite values.
Results may differ from the reference program's by a relative error of at most 0.0085.
Values may be sent and summed in bfloat16 or wider, within the bound.
A program may use at most 192 MiB of HBM per device.

```python
import math
import jax
import jax.numpy as jnp
from jax import lax

HEAD_COUNT = 8
DK = 256
DV = 512
TOK_DEV = 1024
STRETCH = 1024
TOKEN_COUNT = 16384


def draw_values(key, part):
    main_key, column_key = jax.random.split(key, 2)
    column_scale = jnp.exp(jax.random.uniform(column_key, (1, HEAD_COUNT * DV), jnp.float32, 0.0, math.log(10.0)))
    return (jnp.clip(jax.random.normal(main_key, (TOKEN_COUNT, HEAD_COUNT * DV), jnp.float32), -6.0, 6.0) * column_scale).astype(jnp.bfloat16)


def draw_in_gate(key, part):
    base_key = jax.random.fold_in(key, 0)
    return jax.random.uniform(base_key, (TOKEN_COUNT, HEAD_COUNT), jnp.float32, -4.0, 3.0).astype(jnp.bfloat16)


def draw_forget_gate(key, part):
    rank_random_key, quick_random_key, device_random_key, coarse_random_key, spike_random_key, loss_random_key = jax.random.split(key, 6)
    rank = jax.random.permutation(rank_random_key, HEAD_COUNT)
    slow_count = HEAD_COUNT // 2
    middle_count = HEAD_COUNT // 4
    fast_rate = jnp.exp(jax.random.uniform(quick_random_key, (HEAD_COUNT,), jnp.float32, math.log(1.0 / 50.0), math.log(1.0 / 30.0)))
    base_rate = jnp.where(rank < slow_count, 0.3 / TOKEN_COUNT, jnp.where(rank < slow_count + middle_count, 2.0 / TOK_DEV, fast_rate))
    shard_factor = jnp.exp(jax.random.uniform(device_random_key, (TOKEN_COUNT // TOK_DEV, 1, HEAD_COUNT), jnp.float32, -math.log(2.0), math.log(2.0)))
    shard_factor = jnp.broadcast_to(shard_factor, (TOKEN_COUNT // TOK_DEV, TOK_DEV, HEAD_COUNT)).reshape(TOKEN_COUNT, HEAD_COUNT)
    rough = jnp.exp(jax.random.uniform(coarse_random_key, (TOKEN_COUNT, HEAD_COUNT), jnp.float32, -0.35, 0.35))
    rate = base_rate[None, :] * shard_factor * rough
    spike_location = jax.random.randint(spike_random_key, (2, HEAD_COUNT), 0, TOKEN_COUNT)
    loss = jax.random.uniform(loss_random_key, (2, HEAD_COUNT), jnp.float32, 0.2, 0.5)
    token_position = jnp.arange(TOKEN_COUNT, dtype=jnp.int32)[:, None, None]
    spike_hit_mask = token_position == spike_location[None]
    rate = rate + jnp.sum(jnp.where(spike_hit_mask, -jnp.log(1.0 - loss)[None], 0.0), axis=1)
    return (-rate - jnp.log(-jnp.expm1(-rate))).astype(jnp.bfloat16)


def levels(rng, extent, cuts, least, high):
    level = 1.0
    for dim, blocks in cuts:
        steps = jax.random.uniform(jax.random.fold_in(jax.random.fold_in(rng, 6), dim), (blocks,), jnp.float32, least / len(cuts), high / len(cuts))
        level = level * jnp.repeat(jnp.exp(steps), extent[dim] // blocks).reshape((-1,) + (1,) * (len(extent) - 1 - dim))
    return level


def centred(rng, extent, deviation, bound, cuts=(), held_as=jnp.bfloat16):
    factor_of = levels(rng, extent, cuts, -0.22, 0.18) if cuts else 1.0
    values = jax.random.normal(rng, extent, jnp.float32) * deviation * factor_of
    return jnp.minimum(jnp.maximum(values, -bound), bound).astype(held_as)


def setup_inputs(seed: int = 0) -> dict:
    arg_keys = jax.random.split(jax.random.key(seed), 8)
    return {
        "queries": centred(arg_keys[0], (TOKEN_COUNT, HEAD_COUNT * DK), 1.0, 6.0, ((0, 32),)),
        "key_rows": centred(arg_keys[1], (TOKEN_COUNT, HEAD_COUNT * DK), 1.0, 6.0, ((0, 32),)),
        "values": draw_values(jax.random.fold_in(arg_keys[7], 71), 0),
        "in_gate": draw_in_gate(jax.random.fold_in(arg_keys[7], 71), 0),
        "forget_gate": draw_forget_gate(jax.random.fold_in(arg_keys[7], 71), 0),
        "out_gate": centred(arg_keys[5], (TOKEN_COUNT, HEAD_COUNT * DV), 1.0, 6.0, ((0, 32),)),
        "norm_gain": jnp.clip(1.0 + 0.18 * jax.random.normal(arg_keys[6], (HEAD_COUNT * DV,), jnp.float32), 0.1, 1.9),
    }


far_below = -1e+30
norm_eps = 1e-06

def combine(earlier, later):
    state_a, max_a, decay_a = earlier
    state_b, max_b, decay_b = later
    shifted = max_a + decay_b
    joint_max = jnp.maximum(shifted, max_b)
    state_total_sum = jnp.exp(shifted - joint_max)[..., None, None] * state_a + jnp.exp(max_b - joint_max)[..., None, None] * state_b
    return (state_total_sum, joint_max, decay_a + decay_b)

def summarize(keys_blk, values_block, in_blk, forget_blk):
    log_forget = jax.nn.log_sigmoid(forget_blk.astype(jnp.float32))
    running = jnp.cumsum(log_forget, axis=0)
    final_cum = running[-1]
    log_weight = final_cum[None, :] - running + in_blk.astype(jnp.float32)
    block_max = lax.optimization_barrier(jnp.max(log_weight, axis=0))
    weighted_values = (jnp.exp(log_weight - block_max[None, :])[:, :, None] * keys_blk.astype(jnp.float32)).astype(jnp.bfloat16)
    weighted_values = lax.optimization_barrier(weighted_values).astype(jnp.float32)
    state_total_sum = jnp.einsum('yij,yip->ijp', weighted_values, values_block.astype(jnp.float32))
    return (running, (state_total_sum, block_max, final_cum))

def block_output(query_block, keys_blk, values_block, in_blk, running, prefix):
    prefix_state = prefix[0]
    prefix_max = prefix[1]
    scores = jnp.einsum('thk,shk->hts', query_block.astype(jnp.float32), keys_blk.astype(jnp.float32))
    cum_rows = running.T
    input_rows = in_blk.astype(jnp.float32).T
    log_weight = cum_rows[:, :, None] - cum_rows[:, None, :] + input_rows[:, None, :]
    span_rows = running.shape[0]
    causal = lax.broadcasted_iota(jnp.int32, (span_rows, span_rows), 0) >= lax.broadcasted_iota(jnp.int32, (span_rows, span_rows), 1)
    log_weight = jnp.where(causal[None], log_weight, -jnp.inf)
    carried = cum_rows + prefix_max[:, None]
    row_max = jnp.maximum(carried, lax.optimization_barrier(jnp.max(log_weight, axis=2)))
    mixed_weights = (scores * jnp.exp(log_weight - row_max[:, :, None])).astype(jnp.bfloat16)
    mixed_weights = lax.optimization_barrier(mixed_weights).astype(jnp.float32)
    within = jnp.einsum('hts,shv->thv', mixed_weights, values_block.astype(jnp.float32))
    state_bfloat = lax.optimization_barrier(prefix_state.astype(jnp.bfloat16)).astype(jnp.float32)
    preceding_portion = jnp.einsum('ydw,dwl->ydl', query_block.astype(jnp.float32), state_bfloat)
    return within + jnp.exp(carried - row_max).T[:, :, None] * preceding_portion

def reference(queries, key_rows, values, in_gate, forget_gate, out_gate, norm_gain):
    blocks = TOKEN_COUNT // STRETCH
    pieces = (queries.reshape(blocks, STRETCH, HEAD_COUNT, DK), key_rows.reshape(blocks, STRETCH, HEAD_COUNT, DK), values.reshape(blocks, STRETCH, HEAD_COUNT, DV), in_gate.reshape(blocks, STRETCH, HEAD_COUNT), forget_gate.reshape(blocks, STRETCH, HEAD_COUNT))
    initial = (jnp.zeros((HEAD_COUNT, DK, DV), jnp.float32), jnp.full((HEAD_COUNT,), far_below, jnp.float32), jnp.zeros((HEAD_COUNT,), jnp.float32))

    def advance(carry, piece):
        query_block, keys_blk, values_block, in_blk, forget_blk = piece
        running, summary = summarize(keys_blk, values_block, in_blk, forget_blk)
        mixed_blk = block_output(query_block, keys_blk, values_block, in_blk, running, carry)
        return (combine(carry, summary), mixed_blk)
    final_sum, mixed = lax.scan(advance, initial, pieces)
    mixed = mixed.reshape(TOKEN_COUNT, HEAD_COUNT, DV)
    mean_sq = lax.optimization_barrier(jnp.mean(mixed * mixed, axis=-1, keepdims=True))
    normed = (mixed * lax.rsqrt(mean_sq + norm_eps) * norm_gain.reshape(HEAD_COUNT, DV)).astype(jnp.bfloat16)
    normed = lax.optimization_barrier(normed).reshape(TOKEN_COUNT, HEAD_COUNT * DV).astype(jnp.float32)
    return (jax.nn.sigmoid(out_gate.astype(jnp.float32)) * normed).astype(jnp.bfloat16)
```

```python
import functools

import jax
import jax.numpy as jnp
from jax import lax
from jax.experimental import pallas as pl
from jax.experimental.pallas import tpu as pltpu

far_below = -1e30
norm_eps = 1e-06
MESH = pl.DeviceIdType.MESH
F32 = jnp.float32
BF16 = jnp.bfloat16
PIECES = 2


def kernel(
    n, m, H, NP,
    q_hbm, k_hbm, v_hbm, ig_ref, fg_ref, igt_ref, fgt_ref, og_hbm, gain_ref,
    out_hbm,
    q, k, v, og, ob, within, acol, arow, dec, amax, scal_s, scal, mall, e1, e2, alph,
    cm, gain, sb, rb, dbuf, cs, cr, pb, pr,
    in_sem, out_sem, scs, scr, cms, cmr, gs, gr, s1, r1, sc, rc, s3, r3,
):
    T, HK = q.shape
    DK = HK // H
    DV = v.shape[1] // H
    c = H // m
    nA = n // c
    RP = DK // NP
    a = lax.axis_index("seq")
    b = lax.axis_index("head")
    A = a // c
    l = (a % c) * m + b

    loads = [
        pltpu.make_async_copy(src, dst, in_sem.at[i])
        for i, (src, dst) in enumerate(((k_hbm, k), (v_hbm, v), (q_hbm, q), (og_hbm, og)))
    ]
    for ld in loads:
        ld.start()

    def member(lp):
        return (A * c + lp // m, lp % m)

    def other(o):
        return (l + o) % H

    has_prev = A > 0
    has_next = A < nA - 1

    barrier = pltpu.get_barrier_semaphore()
    for o in range(1, H):
        pl.semaphore_signal(barrier, inc=1, device_id=member(other(o)), device_id_type=MESH)

    @pl.when(has_prev)
    def _():
        pl.semaphore_signal(barrier, inc=1, device_id=(a - c, b), device_id_type=MESH)

    @pl.when(has_next)
    def _():
        pl.semaphore_signal(barrier, inc=1, device_id=(a + c, b), device_id_type=MESH)

    rows_i = lax.broadcasted_iota(jnp.int32, (T, T), 0)
    cols_i = lax.broadcasted_iota(jnp.int32, (T, T), 1)
    lower = (rows_i >= cols_i).astype(F32)
    upper = (rows_i <= cols_i).astype(F32)
    lf_col = jax.nn.log_sigmoid(fg_ref[...].astype(F32))
    lf_row = jax.nn.log_sigmoid(fgt_ref[...].astype(F32))
    cum_col = jnp.dot(lower, lf_col, precision=lax.Precision.HIGHEST, preferred_element_type=F32)
    cum_row = jnp.dot(lf_row, upper, precision=lax.Precision.HIGHEST, preferred_element_type=F32)
    a_col = ig_ref[...].astype(F32) - cum_col
    a_row = igt_ref[...].astype(F32) - cum_row
    for h in range(H):
        acol[h] = a_col[:, h : h + 1]
    arow[...] = a_row
    top = jnp.broadcast_to(jnp.max(a_row, axis=1, keepdims=True), (H, 128))
    total = jnp.broadcast_to(cum_row[:, T - 1 : T], (H, 128))
    amax[...] = top
    scal_s[0] = total + top
    scal_s[1] = total
    scal[l, 0] = total + top
    scal[l, 1] = total
    gain[b] = gain_ref[...]

    pl.semaphore_wait(barrier, H - 1 + has_prev.astype(jnp.int32) + has_next.astype(jnp.int32))

    def scal_copy(o, src):
        return pltpu.make_async_remote_copy(
            src_ref=scal_s, dst_ref=scal.at[src], send_sem=scs.at[o], recv_sem=scr.at[src],
            device_id=member(other(o)), device_id_type=MESH)

    def gain_copy(o, src):
        return pltpu.make_async_remote_copy(
            src_ref=gain_ref, dst_ref=gain.at[src], send_sem=gs.at[o], recv_sem=gr.at[src],
            device_id=(a, (b + o) % m), device_id_type=MESH)

    def sum_copy(o, p, src):
        rows = pl.ds(p * RP, RP)
        return pltpu.make_async_remote_copy(
            src_ref=sb.at[other(o), rows], dst_ref=rb.at[src, rows],
            send_sem=s1.at[o, p], recv_sem=r1.at[src, p],
            device_id=member(other(o)), device_id_type=MESH)

    def pre_copy(o, p, src):
        rows = pl.ds(p * RP, RP)
        return pltpu.make_async_remote_copy(
            src_ref=pb.at[other(o), rows], dst_ref=pr.at[src, rows],
            send_sem=s3.at[o, p], recv_sem=r3.at[src, p],
            device_id=member(other(o)), device_id_type=MESH)

    def chain_copy(p):
        rows = pl.ds(p * RP, RP)
        return pltpu.make_async_remote_copy(
            src_ref=cs.at[rows], dst_ref=cr.at[rows], send_sem=sc.at[p], recv_sem=rc.at[p],
            device_id=(a + c, b), device_id_type=MESH)

    def max_copy():
        return pltpu.make_async_remote_copy(
            src_ref=mall.at[H], dst_ref=cm, send_sem=cms, recv_sem=cmr,
            device_id=(a + c, b), device_id_type=MESH)

    for o in range(1, H):
        scal_copy(o, l).start()
    for o in range(1, m):
        gain_copy(o, b).start()

    loads[0].wait()
    loads[1].wait()

    def summary(h):
        kc = pl.ds(pl.multiple_of(h * DK, DK), DK)
        vc = pl.ds(pl.multiple_of(h * DV, DV), DV)
        w = jnp.exp(acol[h] - amax[pl.ds(h, 1), 0:1])
        wk = (w * k[:, kc].astype(F32)).astype(BF16)
        return lax.dot_general(
            wk, v[:, vc], (((0,), (0,)), ((), ())), preferred_element_type=F32
        ).astype(BF16)

    def first_piece(o, carry):
        sb[other(o)] = summary(other(o))
        sum_copy(o, 0, l).start()
        return carry

    lax.fori_loop(1, H, first_piece, 0)
    for p in range(1, NP):
        for o in range(1, H):
            sum_copy(o, p, l).start()
    rb[l] = summary(l)

    for o in range(1, H):
        scal_copy(o, other(o)).wait_recv()

    @pl.when(has_prev)
    def _():
        max_copy().wait_recv()
        mall[0] = cm[...]

    @pl.when(jnp.logical_not(has_prev))
    def _():
        mall[0] = jnp.full((H, 128), far_below, F32)

    al = jnp.ones((H, 128), F32)
    before = mall[0]
    alph[0] = al
    for i in range(H):
        own, decay = scal[i, 0], scal[i, 1]
        shifted = before + decay
        after = jnp.maximum(shifted, own)
        x1 = jnp.exp(shifted - after)
        e1[i] = x1
        e2[i] = jnp.exp(own - after)
        al = al * x1
        alph[i + 1] = al
        mall[i + 1] = after
        before = after

    @pl.when(has_next)
    def _():
        max_copy().start()

    loads[2].wait()
    TB = min(256, T)

    def inner(h, carry):
        kc = pl.ds(pl.multiple_of(h * DK, DK), DK)
        vc = pl.ds(pl.multiple_of(h * DV, DV), DV)
        M = mall[l, pl.ds(h, 1), 0:1]
        for t0 in range(0, T, TB):
            S = t0 + TB
            row = arow[pl.ds(h, 1), 0:S]
            causal = (lax.broadcasted_iota(jnp.int32, (TB, S), 0) + t0) >= (
                lax.broadcasted_iota(jnp.int32, (TB, S), 1))
            lw = jnp.where(causal, jnp.broadcast_to(row, (TB, S)), -jnp.inf)
            r = jnp.maximum(jnp.max(lw, axis=1, keepdims=True), M)
            sco = lax.dot_general(
                q[t0 : t0 + TB, kc], k[0:S, kc], (((1,), (1,)), ((), ())),
                preferred_element_type=F32)
            mix = (sco * jnp.exp(lw - r)).astype(BF16)
            within[t0 : t0 + TB, vc] = jnp.dot(mix, v[0:S, vc], preferred_element_type=F32)
            dec[h, t0 : t0 + TB] = jnp.exp(M - r)
        return carry

    lax.fori_loop(0, H, inner, 0)

    for p in range(NP):
        rows = slice(p * RP, (p + 1) * RP)
        for o in range(1, H):
            sum_copy(o, p, other(o)).wait_recv()
        one = pl.ds(l, 1)
        dbuf[0] = jnp.zeros((RP, DV), F32)
        for i in range(H):
            dbuf[i + 1] = e1[i, one, 0:1] * dbuf[i] + e2[i, one, 0:1] * rb[i, rows].astype(F32)

        @pl.when(has_prev)
        def _():
            chain_copy(p).wait_recv()

        @pl.when(jnp.logical_not(has_prev))
        def _():
            cr[rows] = jnp.zeros((RP, DV), BF16)

        @pl.when(has_next)
        def _():
            cs[rows] = (alph[H, one, 0:1] * cr[rows].astype(F32) + dbuf[H]).astype(BF16)
            chain_copy(p).start()

        for i in range(H):
            pb[i, rows] = (alph[i, one, 0:1] * cr[rows].astype(F32) + dbuf[i]).astype(BF16)
        for o in range(1, H):
            pre_copy(o, p, l).start()
        pr[l, rows] = pb[l, rows]

    loads[3].wait()
    for o in range(1, m):
        gain_copy(o, (b + o) % m).wait_recv()

    def out_copy(h):
        vc = pl.ds(pl.multiple_of(h * DV, DV), DV)
        return pltpu.make_async_copy(ob.at[:, vc], out_hbm.at[:, vc], out_sem.at[h])

    def finish(o, carry):
        h = other(o)

        @pl.when(o > 0)
        def _():
            for p in range(NP):
                pre_copy(o, p, h).wait_recv()

        kc = pl.ds(pl.multiple_of(h * DK, DK), DK)
        vc = pl.ds(pl.multiple_of(h * DV, DV), DV)
        g = gain[h // c, :, pl.ds(pl.multiple_of((h % c) * DV, DV), DV)]
        for t0 in range(0, T, TB):
            ts = slice(t0, t0 + TB)
            early = jnp.dot(q[ts, kc], pr[h], preferred_element_type=F32)
            mixed = within[ts, vc] + dec[h, ts] * early
            ms = jnp.mean(mixed * mixed, axis=1, keepdims=True)
            normed = (mixed * lax.rsqrt(ms + norm_eps) * g).astype(BF16)
            gate = jax.nn.sigmoid(og[ts, vc].astype(F32))
            ob[ts, vc] = (gate * normed.astype(F32)).astype(BF16)
        out_copy(h).start()
        return carry

    lax.fori_loop(0, H, finish, 0)

    for h in range(H):
        out_copy(h).wait()
    for o in range(1, H):
        scal_copy(o, l).wait_send()
        for p in range(NP):
            sum_copy(o, p, l).wait_send()
            pre_copy(o, p, l).wait_send()
    for o in range(1, m):
        gain_copy(o, b).wait_send()

    @pl.when(has_next)
    def _():
        max_copy().wait_send()
        for p in range(NP):
            chain_copy(p).wait_send()


def local(n, m, queries, key_rows, values, in_gate, forget_gate, out_gate, norm_gain):
    T, H = in_gate.shape
    HK = queries.shape[1]
    HV = values.shape[1]
    DK, DV = HK // H, HV // H
    NP = PIECES
    RP = DK // NP
    any_ = pl.BlockSpec(memory_space=pl.ANY)
    vm = pl.BlockSpec(memory_space=pltpu.VMEM)
    V = pltpu.VMEM
    D = pltpu.SemaphoreType.DMA
    gain2 = norm_gain.reshape(1, -1)
    return pl.pallas_call(
        functools.partial(kernel, n, m, H, NP),
        out_shape=jax.ShapeDtypeStruct((T, HV), BF16),
        in_specs=[any_, any_, any_, vm, vm, vm, vm, any_, vm],
        out_specs=any_,
        scratch_shapes=[
            V((T, HK), BF16), V((T, HK), BF16), V((T, HV), BF16), V((T, HV), BF16),
            V((T, HV), BF16), V((T, HV), F32),
            V((H, T, 1), F32), V((H, T), F32), V((H, T, 1), F32), V((H, 128), F32),
            V((2, H, 128), F32), V((H, 2, H, 128), F32), V((H + 1, H, 128), F32),
            V((H, H, 128), F32), V((H, H, 128), F32), V((H + 1, H, 128), F32),
            V((H, 128), F32), V((m, 1, gain2.shape[1]), F32),
            V((H, DK, DV), BF16), V((H, DK, DV), BF16), V((H + 1, RP, DV), F32),
            V((DK, DV), BF16), V((DK, DV), BF16), V((H, DK, DV), BF16), V((H, DK, DV), BF16),
            D((4,)), D((H,)), D((H,)), D((H,)), D, D, D((m,)), D((m,)),
            D((H, NP)), D((H, NP)), D((NP,)), D((NP,)), D((H, NP)), D((H, NP)),
        ],
        compiler_params=pltpu.CompilerParams(
            collective_id=0, has_side_effects=True, vmem_limit_bytes=60 * 1024 * 1024),
    )(queries, key_rows, values, in_gate, forget_gate, in_gate.T, forget_gate.T, out_gate, gain2)


def solution(mesh):
    row = jax.sharding.PartitionSpec(("seq", "head"), None)
    n, m = mesh.shape["seq"], mesh.shape["head"]
    return jax.shard_map(
        functools.partial(local, n, m), mesh=mesh,
        in_specs=(row,) * 6 + (jax.sharding.PartitionSpec("head"),),
        out_specs=row, check_vma=False,
    )
```

```python
import functools

import jax
import jax.numpy as jnp
from jax import lax
from jax.experimental import pallas as pl
from jax.experimental.pallas import tpu as pltpu

far_below = -1e30
norm_eps = 1e-06
MESH = pl.DeviceIdType.MESH
F32 = jnp.float32
BF16 = jnp.bfloat16
PIECES = 4
AHEAD = 2


def kernel(
    n, m, H, NP,
    q_hbm, k_hbm, v_hbm, igt_ref, fgt_ref, gain_ref,
    out_hbm,
    q, k, v, ob, within, acol, arow, dec, amax, scal_s, scal, mall, e1, e2, alph,
    cm, gain, sb, rb, dbuf, cs, cr, pb, pr,
    in_sem, kv_sem, out_sem, scs, scr, cms, cmr, gs, gr, s1, r1, sc, rc, s3, r3,
):
    T, HK = q.shape
    DK = HK // H
    DV = v.shape[1] // H
    c = H // m
    nA = n // c
    RP = DK // NP
    a = lax.axis_index("seq")
    b = lax.axis_index("head")
    A = a // c
    l = (a % c) * m + b

    def member(lp):
        return (A * c + lp // m, lp % m)

    def other(o):
        return (l + o) % H

    def head_loads(o):
        h = other(o)
        kc = pl.ds(pl.multiple_of(h * DK, DK), DK)
        vc = pl.ds(pl.multiple_of(h * DV, DV), DV)
        return (
            pltpu.make_async_copy(k_hbm.at[:, kc], k.at[:, kc], kv_sem.at[o, 0]),
            pltpu.make_async_copy(v_hbm.at[:, vc], v.at[:, vc], kv_sem.at[o, 1]),
        )

    for o in (*range(1, H), 0):
        for ld in head_loads(o):
            ld.start()
    q_load = pltpu.make_async_copy(q_hbm, q, in_sem)
    q_load.start()

    has_prev = A > 0
    has_next = A < nA - 1

    barrier = pltpu.get_barrier_semaphore()
    for o in range(1, H):
        pl.semaphore_signal(barrier, inc=1, device_id=member(other(o)), device_id_type=MESH)

    @pl.when(has_prev)
    def _():
        pl.semaphore_signal(barrier, inc=1, device_id=(a - c, b), device_id_type=MESH)

    @pl.when(has_next)
    def _():
        pl.semaphore_signal(barrier, inc=1, device_id=(a + c, b), device_id_type=MESH)

    rows_i = lax.broadcasted_iota(jnp.int32, (T, T), 0)
    cols_i = lax.broadcasted_iota(jnp.int32, (T, T), 1)
    upper = (rows_i <= cols_i).astype(F32)
    lf_row = jax.nn.log_sigmoid(fgt_ref[...].astype(F32))
    cum_row = jnp.dot(lf_row, upper, precision=lax.Precision.HIGHEST, preferred_element_type=F32)
    a_row = igt_ref[...].astype(F32) - cum_row
    a_col = a_row.T
    for h in range(H):
        acol[h] = a_col[:, h : h + 1]
    arow[...] = a_row
    top = jnp.broadcast_to(jnp.max(a_row, axis=1, keepdims=True), (H, 128))
    total = jnp.broadcast_to(cum_row[:, T - 1 : T], (H, 128))
    amax[...] = top
    scal_s[0] = total + top
    scal_s[1] = total
    scal[l, 0] = total + top
    scal[l, 1] = total
    gain[b] = gain_ref[...]

    pl.semaphore_wait(barrier, H - 1 + has_prev.astype(jnp.int32) + has_next.astype(jnp.int32))

    def scal_copy(o, src):
        return pltpu.make_async_remote_copy(
            src_ref=scal_s, dst_ref=scal.at[src], send_sem=scs.at[o], recv_sem=scr.at[src],
            device_id=member(other(o)), device_id_type=MESH)

    def gain_copy(o, src):
        return pltpu.make_async_remote_copy(
            src_ref=gain_ref, dst_ref=gain.at[src], send_sem=gs.at[o], recv_sem=gr.at[src],
            device_id=(a, (b + o) % m), device_id_type=MESH)

    def sum_copy(o, p, src):
        rows = pl.ds(p * RP, RP)
        return pltpu.make_async_remote_copy(
            src_ref=sb.at[other(o), rows], dst_ref=rb.at[src, rows],
            send_sem=s1.at[o, p], recv_sem=r1.at[src, p],
            device_id=member(other(o)), device_id_type=MESH)

    def pre_copy(o, p, src):
        rows = pl.ds(p * RP, RP)
        return pltpu.make_async_remote_copy(
            src_ref=pb.at[other(o), rows], dst_ref=pr.at[src, rows],
            send_sem=s3.at[o, p], recv_sem=r3.at[src, p],
            device_id=member(other(o)), device_id_type=MESH)

    def chain_copy(p):
        rows = pl.ds(p * RP, RP)
        return pltpu.make_async_remote_copy(
            src_ref=cs.at[rows], dst_ref=cr.at[rows], send_sem=sc.at[p], recv_sem=rc.at[p],
            device_id=(a + c, b), device_id_type=MESH)

    def max_copy():
        return pltpu.make_async_remote_copy(
            src_ref=mall.at[H], dst_ref=cm, send_sem=cms, recv_sem=cmr,
            device_id=(a + c, b), device_id_type=MESH)

    for o in range(1, H):
        scal_copy(o, l).start()
    for o in range(1, m):
        gain_copy(o, b).start()

    def summary(h):
        kc = pl.ds(pl.multiple_of(h * DK, DK), DK)
        vc = pl.ds(pl.multiple_of(h * DV, DV), DV)
        w = jnp.exp(acol[h] - amax[pl.ds(h, 1), 0:1])
        wk = (w * k[:, kc].astype(F32)).astype(BF16)
        return lax.dot_general(
            wk, v[:, vc], (((0,), (0,)), ((), ())), preferred_element_type=F32
        ).astype(BF16)

    def first_piece(o, carry):
        for ld in head_loads(o):
            ld.wait()
        sb[other(o)] = summary(other(o))
        sum_copy(o, 0, l).start()
        return carry

    lax.fori_loop(1, H, first_piece, 0)
    for p in range(1, NP):
        for o in range(1, H):
            sum_copy(o, p, l).start()
    for ld in head_loads(0):
        ld.wait()
    rb[l] = summary(l)

    for o in range(1, H):
        scal_copy(o, other(o)).wait_recv()

    @pl.when(has_prev)
    def _():
        max_copy().wait_recv()
        mall[0] = cm[...]

    @pl.when(jnp.logical_not(has_prev))
    def _():
        mall[0] = jnp.full((H, 128), far_below, F32)

    al = jnp.ones((H, 128), F32)
    before = mall[0]
    alph[0] = al
    for i in range(H):
        own, decay = scal[i, 0], scal[i, 1]
        shifted = before + decay
        after = jnp.maximum(shifted, own)
        x1 = jnp.exp(shifted - after)
        e1[i] = x1
        e2[i] = jnp.exp(own - after)
        al = al * x1
        alph[i + 1] = al
        mall[i + 1] = after
        before = after

    @pl.when(has_next)
    def _():
        max_copy().start()

    q_load.wait()
    TB = min(256, T)

    def inner(h, carry):
        kc = pl.ds(pl.multiple_of(h * DK, DK), DK)
        vc = pl.ds(pl.multiple_of(h * DV, DV), DV)
        M = mall[l, pl.ds(h, 1), 0:1]
        for t0 in range(0, T, TB):
            S = t0 + TB
            row = arow[pl.ds(h, 1), 0:S]
            causal = (lax.broadcasted_iota(jnp.int32, (TB, S), 0) + t0) >= (
                lax.broadcasted_iota(jnp.int32, (TB, S), 1))
            lw = jnp.where(causal, jnp.broadcast_to(row, (TB, S)), -jnp.inf)
            r = jnp.maximum(jnp.max(lw, axis=1, keepdims=True), M)
            sco = lax.dot_general(
                q[t0 : t0 + TB, kc], k[0:S, kc], (((1,), (1,)), ((), ())),
                preferred_element_type=F32)
            mix = (sco * jnp.exp(lw - r)).astype(BF16)
            within[t0 : t0 + TB, vc] = jnp.dot(mix, v[0:S, vc], preferred_element_type=F32)
            dec[h, t0 : t0 + TB] = jnp.exp(M - r)
        return carry

    lax.fori_loop(0, AHEAD, inner, 0)

    for p in range(NP):
        rows = slice(p * RP, (p + 1) * RP)
        for o in range(1, H):
            sum_copy(o, p, other(o)).wait_recv()
        one = pl.ds(l, 1)
        dbuf[0] = jnp.zeros((RP, DV), F32)
        for i in range(H):
            dbuf[i + 1] = e1[i, one, 0:1] * dbuf[i] + e2[i, one, 0:1] * rb[i, rows].astype(F32)

        @pl.when(has_prev)
        def _():
            chain_copy(p).wait_recv()

        @pl.when(jnp.logical_not(has_prev))
        def _():
            cr[rows] = jnp.zeros((RP, DV), BF16)

        @pl.when(has_next)
        def _():
            cs[rows] = (alph[H, one, 0:1] * cr[rows].astype(F32) + dbuf[H]).astype(BF16)
            chain_copy(p).start()

        for i in range(H):
            pb[i, rows] = (alph[i, one, 0:1] * cr[rows].astype(F32) + dbuf[i]).astype(BF16)
        for o in range(1, H):
            pre_copy(o, p, l).start()
        pr[l, rows] = pb[l, rows]

    lax.fori_loop(AHEAD, H, inner, 0)

    for o in range(1, m):
        gain_copy(o, (b + o) % m).wait_recv()

    def out_copy(h):
        vc = pl.ds(pl.multiple_of(h * DV, DV), DV)
        return pltpu.make_async_copy(ob.at[:, vc], out_hbm.at[:, vc], out_sem.at[h])

    def finish(o, carry):
        h = other(H - o)

        @pl.when(o > 0)
        def _():
            for p in range(NP):
                pre_copy(o, p, h).wait_recv()

        kc = pl.ds(pl.multiple_of(h * DK, DK), DK)
        vc = pl.ds(pl.multiple_of(h * DV, DV), DV)
        g = gain[h // c, :, pl.ds(pl.multiple_of((h % c) * DV, DV), DV)]
        for t0 in range(0, T, TB):
            ts = slice(t0, t0 + TB)
            early = jnp.dot(q[ts, kc], pr[h], preferred_element_type=F32)
            mixed = within[ts, vc] + dec[h, ts] * early
            ms = jnp.mean(mixed * mixed, axis=1, keepdims=True)
            ob[ts, vc] = (mixed * lax.rsqrt(ms + norm_eps) * g).astype(BF16)
        out_copy(h).start()
        return carry

    lax.fori_loop(0, H, finish, 0)

    for h in range(H):
        out_copy(h).wait()
    for o in range(1, H):
        scal_copy(o, l).wait_send()
        for p in range(NP):
            sum_copy(o, p, l).wait_send()
            pre_copy(o, p, l).wait_send()
    for o in range(1, m):
        gain_copy(o, b).wait_send()

    @pl.when(has_next)
    def _():
        max_copy().wait_send()
        for p in range(NP):
            chain_copy(p).wait_send()


def local(n, m, queries, key_rows, values, in_gate, forget_gate, out_gate, norm_gain):
    T, H = in_gate.shape
    HK = queries.shape[1]
    HV = values.shape[1]
    DK, DV = HK // H, HV // H
    NP = PIECES
    RP = DK // NP
    any_ = pl.BlockSpec(memory_space=pl.ANY)
    vm = pl.BlockSpec(memory_space=pltpu.VMEM)
    V = pltpu.VMEM
    D = pltpu.SemaphoreType.DMA
    gain2 = norm_gain.reshape(1, -1)
    normed = pl.pallas_call(
        functools.partial(kernel, n, m, H, NP),
        out_shape=jax.ShapeDtypeStruct((T, HV), BF16),
        in_specs=[any_, any_, any_, vm, vm, vm],
        out_specs=any_,
        scratch_shapes=[
            V((T, HK), BF16), V((T, HK), BF16), V((T, HV), BF16),
            V((T, HV), BF16), V((T, HV), F32),
            V((H, T, 1), F32), V((H, T), F32), V((H, T, 1), F32), V((H, 128), F32),
            V((2, H, 128), F32), V((H, 2, H, 128), F32), V((H + 1, H, 128), F32),
            V((H, H, 128), F32), V((H, H, 128), F32), V((H + 1, H, 128), F32),
            V((H, 128), F32), V((m, 1, gain2.shape[1]), F32),
            V((H, DK, DV), BF16), V((H, DK, DV), BF16), V((H + 1, RP, DV), F32),
            V((DK, DV), BF16), V((DK, DV), BF16), V((H, DK, DV), BF16), V((H, DK, DV), BF16),
            D, D((H, 2)), D((H,)), D((H,)), D((H,)), D, D, D((m,)), D((m,)),
            D((H, NP)), D((H, NP)), D((NP,)), D((NP,)), D((H, NP)), D((H, NP)),
        ],
        compiler_params=pltpu.CompilerParams(
            collective_id=0, has_side_effects=True, vmem_limit_bytes=60 * 1024 * 1024),
    )(queries, key_rows, values, in_gate.T, forget_gate.T, gain2)
    return (jax.nn.sigmoid(out_gate.astype(F32)) * normed.astype(F32)).astype(BF16)


def solution(mesh):
    row = jax.sharding.PartitionSpec(("seq", "head"), None)
    n, m = mesh.shape["seq"], mesh.shape["head"]
    return jax.shard_map(
        functools.partial(local, n, m), mesh=mesh,
        in_specs=(row,) * 6 + (jax.sharding.PartitionSpec("head"),),
        out_specs=row, check_vma=False,
    )
```

```python
import functools

import jax
import jax.numpy as jnp
from jax import lax
from jax.experimental import pallas as pl
from jax.experimental.pallas import tpu as pltpu

far_below = -1e30
norm_eps = 1e-06
MESH = pl.DeviceIdType.MESH
F32 = jnp.float32
BF16 = jnp.bfloat16
PIECES = 4
AHEAD = 2


def kernel(
    n, m, H, NP,
    q_hbm, k_hbm, v_hbm, igt_hbm, fgt_hbm, gain_hbm,
    out_hbm,
    q, k, v, ob, within, acol, arow, dec, amax, scal_s, scal, mall, e1, e2, alph,
    cm, gain, sb, rb, dbuf, cs, cr, pb, pr,
    igt_ref, fgt_ref, gain_ref, small_sem, in_sem, kv_sem, out_sem, scs, scr, cms, cmr, gs, gr, s1, r1, sc, rc, s3, r3,
):
    T, HK = q.shape
    DK = HK // H
    DV = v.shape[1] // H
    c = H // m
    nA = n // c
    RP = DK // NP
    a = lax.axis_index("seq")
    b = lax.axis_index("head")
    A = a // c
    l = (a % c) * m + b

    def member(lp):
        return (A * c + lp // m, lp % m)

    def other(o):
        return (l + o) % H

    def head_loads(o):
        h = other(o)
        kc = pl.ds(pl.multiple_of(h * DK, DK), DK)
        vc = pl.ds(pl.multiple_of(h * DV, DV), DV)
        return (
            pltpu.make_async_copy(k_hbm.at[:, kc], k.at[:, kc], kv_sem.at[o, 0]),
            pltpu.make_async_copy(v_hbm.at[:, vc], v.at[:, vc], kv_sem.at[o, 1]),
        )

    small = [
        pltpu.make_async_copy(src, dst, small_sem.at[i])
        for i, (src, dst) in enumerate(
            ((fgt_hbm, fgt_ref), (igt_hbm, igt_ref), (gain_hbm, gain_ref)))
    ]
    for ld in small:
        ld.start()
    for o in (*range(1, H), 0):
        for ld in head_loads(o):
            ld.start()
    q_load = pltpu.make_async_copy(q_hbm, q, in_sem)
    q_load.start()

    has_prev = A > 0
    has_next = A < nA - 1

    barrier = pltpu.get_barrier_semaphore()
    for o in range(1, H):
        pl.semaphore_signal(barrier, inc=1, device_id=member(other(o)), device_id_type=MESH)

    @pl.when(has_prev)
    def _():
        pl.semaphore_signal(barrier, inc=1, device_id=(a - c, b), device_id_type=MESH)

    @pl.when(has_next)
    def _():
        pl.semaphore_signal(barrier, inc=1, device_id=(a + c, b), device_id_type=MESH)

    for ld in small:
        ld.wait()
    rows_i = lax.broadcasted_iota(jnp.int32, (T, T), 0)
    cols_i = lax.broadcasted_iota(jnp.int32, (T, T), 1)
    upper = (rows_i <= cols_i).astype(F32)
    lf_row = jax.nn.log_sigmoid(fgt_ref[...].astype(F32))
    cum_row = jnp.dot(lf_row, upper, precision=lax.Precision.HIGHEST, preferred_element_type=F32)
    a_row = igt_ref[...].astype(F32) - cum_row
    a_col = a_row.T
    for h in range(H):
        acol[h] = a_col[:, h : h + 1]
    arow[...] = a_row
    top = jnp.broadcast_to(jnp.max(a_row, axis=1, keepdims=True), (H, 128))
    total = jnp.broadcast_to(cum_row[:, T - 1 : T], (H, 128))
    amax[...] = top
    scal_s[0] = total + top
    scal_s[1] = total
    scal[l, 0] = total + top
    scal[l, 1] = total
    gain[b] = gain_ref[...]

    pl.semaphore_wait(barrier, H - 1 + has_prev.astype(jnp.int32) + has_next.astype(jnp.int32))

    def scal_copy(o, src):
        return pltpu.make_async_remote_copy(
            src_ref=scal_s, dst_ref=scal.at[src], send_sem=scs.at[o], recv_sem=scr.at[src],
            device_id=member(other(o)), device_id_type=MESH)

    def gain_copy(o, src):
        return pltpu.make_async_remote_copy(
            src_ref=gain_ref, dst_ref=gain.at[src], send_sem=gs.at[o], recv_sem=gr.at[src],
            device_id=(a, (b + o) % m), device_id_type=MESH)

    def sum_copy(o, p, src):
        rows = pl.ds(p * RP, RP)
        return pltpu.make_async_remote_copy(
            src_ref=sb.at[other(o), rows], dst_ref=rb.at[src, rows],
            send_sem=s1.at[o, p], recv_sem=r1.at[src, p],
            device_id=member(other(o)), device_id_type=MESH)

    def pre_copy(o, p, src):
        rows = pl.ds(p * RP, RP)
        return pltpu.make_async_remote_copy(
            src_ref=pb.at[other(o), rows], dst_ref=pr.at[src, rows],
            send_sem=s3.at[o, p], recv_sem=r3.at[src, p],
            device_id=member(other(o)), device_id_type=MESH)

    def chain_copy(p):
        rows = pl.ds(p * RP, RP)
        return pltpu.make_async_remote_copy(
            src_ref=cs.at[rows], dst_ref=cr.at[rows], send_sem=sc.at[p], recv_sem=rc.at[p],
            device_id=(a + c, b), device_id_type=MESH)

    def max_copy():
        return pltpu.make_async_remote_copy(
            src_ref=mall.at[H], dst_ref=cm, send_sem=cms, recv_sem=cmr,
            device_id=(a + c, b), device_id_type=MESH)

    for o in range(1, H):
        scal_copy(o, l).start()
    for o in range(1, m):
        gain_copy(o, b).start()

    def summary(h):
        kc = pl.ds(pl.multiple_of(h * DK, DK), DK)
        vc = pl.ds(pl.multiple_of(h * DV, DV), DV)
        w = jnp.exp(acol[h] - amax[pl.ds(h, 1), 0:1])
        wk = (w * k[:, kc].astype(F32)).astype(BF16)
        return lax.dot_general(
            wk, v[:, vc], (((0,), (0,)), ((), ())), preferred_element_type=F32
        ).astype(BF16)

    def first_piece(o, carry):
        for ld in head_loads(o):
            ld.wait()
        sb[other(o)] = summary(other(o))
        sum_copy(o, 0, l).start()
        return carry

    lax.fori_loop(1, H, first_piece, 0)
    for p in range(1, NP):
        for o in range(1, H):
            sum_copy(o, p, l).start()
    for ld in head_loads(0):
        ld.wait()
    rb[l] = summary(l)

    for o in range(1, H):
        scal_copy(o, other(o)).wait_recv()

    @pl.when(has_prev)
    def _():
        max_copy().wait_recv()
        mall[0] = cm[...]

    @pl.when(jnp.logical_not(has_prev))
    def _():
        mall[0] = jnp.full((H, 128), far_below, F32)

    al = jnp.ones((H, 128), F32)
    before = mall[0]
    alph[0] = al
    for i in range(H):
        own, decay = scal[i, 0], scal[i, 1]
        shifted = before + decay
        after = jnp.maximum(shifted, own)
        x1 = jnp.exp(shifted - after)
        e1[i] = x1
        e2[i] = jnp.exp(own - after)
        al = al * x1
        alph[i + 1] = al
        mall[i + 1] = after
        before = after

    @pl.when(has_next)
    def _():
        max_copy().start()

    q_load.wait()
    TB = min(256, T)

    def inner(h, carry):
        kc = pl.ds(pl.multiple_of(h * DK, DK), DK)
        vc = pl.ds(pl.multiple_of(h * DV, DV), DV)
        M = mall[l, pl.ds(h, 1), 0:1]
        for t0 in range(0, T, TB):
            S = t0 + TB
            row = arow[pl.ds(h, 1), 0:S]
            causal = (lax.broadcasted_iota(jnp.int32, (TB, S), 0) + t0) >= (
                lax.broadcasted_iota(jnp.int32, (TB, S), 1))
            lw = jnp.where(causal, jnp.broadcast_to(row, (TB, S)), -jnp.inf)
            r = jnp.maximum(jnp.max(lw, axis=1, keepdims=True), M)
            sco = lax.dot_general(
                q[t0 : t0 + TB, kc], k[0:S, kc], (((1,), (1,)), ((), ())),
                preferred_element_type=F32)
            mix = (sco * jnp.exp(lw - r)).astype(BF16)
            within[t0 : t0 + TB, vc] = jnp.dot(mix, v[0:S, vc], preferred_element_type=F32)
            dec[h, t0 : t0 + TB] = jnp.exp(M - r)
        return carry

    lax.fori_loop(0, AHEAD, inner, 0)

    for p in range(NP):
        rows = slice(p * RP, (p + 1) * RP)
        for o in range(1, H):
            sum_copy(o, p, other(o)).wait_recv()
        one = pl.ds(l, 1)
        dbuf[0] = jnp.zeros((RP, DV), F32)
        for i in range(H):
            dbuf[i + 1] = e1[i, one, 0:1] * dbuf[i] + e2[i, one, 0:1] * rb[i, rows].astype(F32)

        @pl.when(has_prev)
        def _():
            chain_copy(p).wait_recv()

        @pl.when(jnp.logical_not(has_prev))
        def _():
            cr[rows] = jnp.zeros((RP, DV), BF16)

        @pl.when(has_next)
        def _():
            cs[rows] = (alph[H, one, 0:1] * cr[rows].astype(F32) + dbuf[H]).astype(BF16)
            chain_copy(p).start()

        for i in range(H):
            pb[i, rows] = (alph[i, one, 0:1] * cr[rows].astype(F32) + dbuf[i]).astype(BF16)
        for o in range(1, H):
            pre_copy(o, p, l).start()
        pr[l, rows] = pb[l, rows]

    lax.fori_loop(AHEAD, H, inner, 0)

    for o in range(1, m):
        gain_copy(o, (b + o) % m).wait_recv()

    def out_copy(h):
        vc = pl.ds(pl.multiple_of(h * DV, DV), DV)
        return pltpu.make_async_copy(ob.at[:, vc], out_hbm.at[:, vc], out_sem.at[h])

    def finish(o, carry):
        h = other(H - o)

        @pl.when(o > 0)
        def _():
            for p in range(NP):
                pre_copy(o, p, h).wait_recv()

        kc = pl.ds(pl.multiple_of(h * DK, DK), DK)
        vc = pl.ds(pl.multiple_of(h * DV, DV), DV)
        g = gain[h // c, :, pl.ds(pl.multiple_of((h % c) * DV, DV), DV)]
        for t0 in range(0, T, TB):
            ts = slice(t0, t0 + TB)
            early = jnp.dot(q[ts, kc], pr[h], preferred_element_type=F32)
            mixed = within[ts, vc] + dec[h, ts] * early
            ms = jnp.mean(mixed * mixed, axis=1, keepdims=True)
            ob[ts, vc] = (mixed * lax.rsqrt(ms + norm_eps) * g).astype(BF16)
        out_copy(h).start()
        return carry

    lax.fori_loop(0, H, finish, 0)

    for h in range(H):
        out_copy(h).wait()
    for o in range(1, H):
        scal_copy(o, l).wait_send()
        for p in range(NP):
            sum_copy(o, p, l).wait_send()
            pre_copy(o, p, l).wait_send()
    for o in range(1, m):
        gain_copy(o, b).wait_send()

    @pl.when(has_next)
    def _():
        max_copy().wait_send()
        for p in range(NP):
            chain_copy(p).wait_send()


def local(n, m, queries, key_rows, values, in_gate, forget_gate, out_gate, norm_gain):
    T, H = in_gate.shape
    HK = queries.shape[1]
    HV = values.shape[1]
    DK, DV = HK // H, HV // H
    NP = PIECES
    RP = DK // NP
    any_ = pl.BlockSpec(memory_space=pl.ANY)
    vm = pl.BlockSpec(memory_space=pltpu.VMEM)
    V = pltpu.VMEM
    D = pltpu.SemaphoreType.DMA
    gain2 = norm_gain.reshape(1, -1)
    normed = pl.pallas_call(
        functools.partial(kernel, n, m, H, NP),
        out_shape=jax.ShapeDtypeStruct((T, HV), BF16),
        in_specs=[any_] * 6,
        out_specs=any_,
        scratch_shapes=[
            V((T, HK), BF16), V((T, HK), BF16), V((T, HV), BF16),
            V((T, HV), BF16), V((T, HV), F32),
            V((H, T, 1), F32), V((H, T), F32), V((H, T, 1), F32), V((H, 128), F32),
            V((2, H, 128), F32), V((H, 2, H, 128), F32), V((H + 1, H, 128), F32),
            V((H, H, 128), F32), V((H, H, 128), F32), V((H + 1, H, 128), F32),
            V((H, 128), F32), V((m, 1, gain2.shape[1]), F32),
            V((H, DK, DV), BF16), V((H, DK, DV), BF16), V((H + 1, RP, DV), F32),
            V((DK, DV), BF16), V((DK, DV), BF16), V((H, DK, DV), BF16), V((H, DK, DV), BF16),
            V((H, T), BF16), V((H, T), BF16), V(gain2.shape, F32), D((3,)), D, D((H, 2)), D((H,)), D((H,)), D((H,)), D, D, D((m,)), D((m,)),
            D((H, NP)), D((H, NP)), D((NP,)), D((NP,)), D((H, NP)), D((H, NP)),
        ],
        compiler_params=pltpu.CompilerParams(
            collective_id=0, has_side_effects=True, vmem_limit_bytes=38 * 1024 * 1024),
    )(*(pltpu.with_memory_space_constraint(x, pltpu.HBM) for x in (
        queries, key_rows, values, in_gate.T, forget_gate.T, gain2)))
    return (jax.nn.sigmoid(out_gate.astype(F32)) * normed.astype(F32)).astype(BF16)


def solution(mesh):
    row = jax.sharding.PartitionSpec(("seq", "head"), None)
    n, m = mesh.shape["seq"], mesh.shape["head"]
    return jax.shard_map(
        functools.partial(local, n, m), mesh=mesh,
        in_specs=(row,) * 6 + (jax.sharding.PartitionSpec("head"),),
        out_specs=row, check_vma=False,
    )
```
